32 devices in a mesh: dp: 8 (over z, y), row: 2 (over core), col: 2 (over x).
Axes of the slice: x: 2, y: 2, z: 4, core: 2. Of those that a mesh axis runs over, the one named last changes fastest.
Arguments:
- x_in: float32 [4096, 768], P(('dp', 'row'), 'col'), may hold values from -6 to 6
- cotangent: float32 [4096, 768], P(('dp', 'row'), 'col'), may hold values from -6 to 6
- segment_ids: int32 [8, 512], P('dp'), may hold values from 0 to 3, never falling along the last dimension, each value on 1 to 256 neighbouring positions
- norm1_gain: float32 [2, 768], P(None, 'col'), may hold values from 0.3 to 3.7
- norm1_bias: float32 [2, 768], P(None, 'col'), may hold values from -1.5 to 1.5
- norm2_gain: float32 [2, 768], P(None, 'col'), may hold values from 0.3 to 3.7
- norm2_bias: float32 [2, 768], P(None, 'col'), may hold values from -1.5 to 1.5
- w_qkv: bfloat16 [2, 768, 2304], P(None, 'col', 'row'), may hold values from -0.21875 to 0.21875
- b_qkv: float32 [2, 2304], P(None, ('row', 'col')), may hold values from -2.5 to 2.5
- w_up: bfloat16 [2, 768, 3072], P(None, 'col', 'row'), may hold values from -0.21875 to 0.21875
- b_up: float32 [2, 3072], P(None, ('row', 'col')), may hold values from -2.5 to 2.5
- w_out: bfloat16 [2, 768, 768], P(None, ('row', 'col')), may hold values from -0.875 to 0.875
- b_out: float32 [2, 768], P(None, 'col'), may hold values from -1.5 to 1.5
- w_down: bfloat16 [2, 3072, 768], P(None, ('row', 'col')), may hold values from -0.109375 to 0.109375
- b_down: float32 [2, 768], P(None, 'col'), may hold values from -1.5 to 1.5
Outputs:
- y_out: float32 [4096, 768], P(('dp', 'row'), 'col')
- x_grad: float32 [4096, 768], P(('dp', 'row'), 'col')
- g_norm1_gain: float32 [2, 768], P(None, 'col')
- g_norm1_bias: float32 [2, 768], P(None, 'col')
- g_norm2_gain: float32 [2, 768], P(None, 'col')
- g_norm2_bias: float32 [2, 768], P(None, 'col')
- g_w_qkv: float32 [2, 768, 2304], P(None, 'col', 'row')
- g_b_qkv: float32 [2, 2304], P(None, ('row', 'col'))
- g_w_up: float32 [2, 768, 3072], P(None, 'col', 'row')
- g_b_up: float32 [2, 3072], P(None, ('row', 'col'))
- g_w_out: float32 [2, 768, 768], P(None, ('row', 'col'))
- g_b_out: float32 [2, 768], P(None, 'col')
- g_w_down: float32 [2, 3072, 768], P(None, ('row', 'col'))
- g_b_down: float32 [2, 768], P(None, 'col')
The draws below stay inside these ranges and needn't reach their ends.
Inputs may be any that keep to these rules, and one draw needn't show every extreme that they name: `segment_ids`: along a sequence the ids never fall; each of the 4 documents of a sequence holds 1 to 256 tokens, one exactly 256.
All inputs are finite; a program needn't handle non-finite values.
Results may differ from the reference program's by a relative error of at most 0.035.
Values may be sent and summed in bfloat16 or wider, within the bound.
A program may use at most 128 MiB of HBM per device.

```python
import math
import jax
import jax.numpy as jnp
import numpy as np
from jax import lax

D = 768
H = 12
HD = 64
ROT = 16
FF = 3072
SEQ = 512
LAYERS = 2
DOCS = 4
DOC_MOST = 256
SEQS = 8
TOKENS = 4096


def ramp_gain(key):
    place = jnp.arange(D, dtype=jnp.float32) / (D - 1.0)
    low = 0.6
    ratio = 5.0
    noise = jnp.clip(0.05 * jax.random.normal(key, (LAYERS, D), jnp.float32), -0.1, 0.1)
    profile = low * jnp.exp(jnp.log(ratio) * place)
    return (profile[None, :] * (1.0 + noise)).astype(jnp.float32)


def draw_norm1_gain(key, part):
    return ramp_gain(jax.random.fold_in(key, 11))


def draw_norm2_gain(key, part):
    return ramp_gain(jax.random.fold_in(key, 23))


def levels(key, shape, shards, least, top_value):
    gain, own = 1.0, jax.random.fold_in(key, 6)
    for dim, shards_of in shards:
        draws = jnp.exp(jax.random.uniform(jax.random.fold_in(own, dim), (shards_of,), jnp.float32, least / len(shards), top_value / len(shards)))
        gain = gain * jnp.repeat(draws, shape[dim] // shards_of).reshape([-1 if axis == dim else 1 for axis in range(len(shape))])
    return gain


def split_up(count, total, limit, lean):
    loads = [(1 << 20) // math.isqrt(rank ** lean) + 1 for rank in range(2, count + 1)]
    surplus, holding = total - limit - (count - 1), [1] * (count - 1)
    while surplus > 0:
        candidates = [i for i in range(count - 1) if holding[i] < limit]
        mass, remaining = sum([loads[i] for i in candidates]), surplus
        for i in candidates:
            more = min(limit - holding[i], max(1, remaining * loads[i] // mass), surplus)
            holding[i] = holding[i] + more
            surplus = surplus - more
    return np.array([limit] + holding)


def uneven(stream_key, count, total, most, slope):
    if count == 2:
        one = jax.random.randint(stream_key, (), max(1, total - most), min(most, total - 1) + 1)
        return jnp.stack([one, total - one])
    lengths = jnp.asarray(split_up(count, total, most, slope), jnp.int32)
    pairs = (count - 1) // 2
    donor, sink = lengths[1:1 + 2 * pairs:2], lengths[2:2 + 2 * pairs:2]
    room = jnp.minimum(donor - 1, most - sink)
    shifted = jax.random.randint(jax.random.fold_in(stream_key, 1), (pairs,), 0, 1 << 20) % (room + 1)
    lengths = lengths.at[1:1 + 2 * pairs:2].set(donor - shifted).at[2:2 + 2 * pairs:2].set(sink + shifted)
    return lengths[jax.random.permutation(jax.random.fold_in(stream_key, 2), count)]


def scatter_about(key, shape, scale, most, split=(), kind=jnp.bfloat16):
    values = scale * jax.random.normal(key, shape, jnp.float32)
    if split:
        values = values * levels(key, shape, split, -0.22, 0.18)
    return jnp.clip(values, -most, most).astype(kind)


def setup_inputs(seed: int = 0) -> dict:
    key_of = jax.random.split(jax.random.key(seed), 16)
    return {
        "x_in": scatter_about(key_of[0], (TOKENS, D), 1.0, 6.0, ((0, 16), (1, 2)), jnp.float32),
        "cotangent": scatter_about(key_of[1], (TOKENS, D), 1.0, 6.0, ((0, 16), (1, 2)), jnp.float32),
        "segment_ids": jax.vmap(lambda own: jnp.searchsorted(jnp.cumsum(uneven(own, DOCS, SEQ, DOC_MOST, 1)), jnp.arange(SEQ), side="right"))(jax.random.split(key_of[2], SEQS)).reshape((SEQS, SEQ)).astype(jnp.int32),
        "norm1_gain": draw_norm1_gain(jax.random.fold_in(key_of[15], 71), 0),
        "norm1_bias": scatter_about(key_of[4], (LAYERS, D), 0.3, 1.5, ((1, 2),), jnp.float32),
        "norm2_gain": draw_norm2_gain(jax.random.fold_in(key_of[15], 71), 0),
        "norm2_bias": scatter_about(key_of[6], (LAYERS, D), 0.3, 1.5, ((1, 2),), jnp.float32),
        "w_qkv": scatter_about(key_of[7], (LAYERS, D, 3 * D), D ** -0.5, 0.21875, ((1, 2), (2, 2))),
        "b_qkv": scatter_about(key_of[8], (LAYERS, 3 * D), 0.5, 2.5, ((1, 4),), jnp.float32),
        "w_up": scatter_about(key_of[9], (LAYERS, D, FF), D ** -0.5, 0.21875, ((1, 2), (2, 2))),
        "b_up": scatter_about(key_of[10], (LAYERS, FF), 0.5, 2.5, ((1, 4),), jnp.float32),
        "w_out": scatter_about(key_of[11], (LAYERS, D, D), (D // 16) ** -0.5, 0.875, ((1, 4),)),
        "b_out": scatter_about(key_of[12], (LAYERS, D), 0.3, 1.5, ((1, 2),), jnp.float32),
        "w_down": scatter_about(key_of[13], (LAYERS, FF, D), FF ** -0.5, 0.109375, ((1, 4),)),
        "b_down": scatter_about(key_of[14], (LAYERS, D), 0.3, 1.5, ((1, 2),), jnp.float32),
    }


EPS = 1e-05
NEG = -1e+30
SCALE = 0.125
INV_ROOT2 = 0.7071067811865476
INV_ROOT_TWO_PI = 0.3989422804014327

def rope_tables(length):
    half = ROT // 2
    freq = 10000.0 ** (-(jnp.arange(half, dtype=jnp.float32) * 2.0) / ROT)
    angle = jnp.arange(length, dtype=jnp.float32)[:, None] * freq[None, :]
    cosine = jnp.concatenate([jnp.cos(angle), jnp.cos(angle)], axis=1)
    sine = jnp.concatenate([jnp.sin(angle), jnp.sin(angle)], axis=1)
    return (cosine, sine)

def rotate(values, cosine, sine):
    part = values[..., :ROT]
    lower = part[..., :ROT // 2]
    upper = part[..., ROT // 2:]
    turned = jnp.concatenate([-upper, lower], axis=-1)
    moved = part * cosine[:, None, :] + turned * sine[:, None, :]
    return jnp.concatenate([moved, values[..., ROT:]], axis=-1)

def unrotate(grads, cosine, sine):
    part = grads[..., :ROT]
    lower = part[..., :ROT // 2]
    upper = part[..., ROT // 2:]
    turned = jnp.concatenate([upper, -lower], axis=-1)
    moved = part * cosine[:, None, :] + turned * sine[:, None, :]
    return jnp.concatenate([moved, grads[..., ROT:]], axis=-1)

def gelu_exact(values):
    return 0.5 * values * (1.0 + jax.scipy.special.erf(values * INV_ROOT2))

def gelu_slope(values):
    return 0.5 * (1.0 + jax.scipy.special.erf(values * INV_ROOT2)) + values * jnp.exp(-0.5 * values * values) * INV_ROOT_TWO_PI

def make_scores(query, key, allowed):
    scores = jnp.einsum('qhd,khd->hqk', query.astype(jnp.float32), key.astype(jnp.float32)) * SCALE
    return jnp.where(allowed[None], scores, NEG)

def attend(query, key, value, allowed):
    scores = make_scores(query, key, allowed)
    top = lax.optimization_barrier(jnp.max(scores, axis=-1, keepdims=True))
    total = lax.optimization_barrier(jnp.sum(jnp.exp(scores - top), axis=-1, keepdims=True))
    lse = top + jnp.log(total)
    probs = jnp.exp(scores - lse).astype(jnp.bfloat16)
    mixed = jnp.einsum('hqk,khd->qhd', probs.astype(jnp.float32), value.astype(jnp.float32))
    return (mixed.astype(jnp.bfloat16), lse)

def attend_back(query, key, value, mixed, grad_mixed, lse, allowed):
    scores = make_scores(query, key, allowed)
    probs = jnp.exp(scores - lse)
    delta = jnp.einsum('qhd,qhd->hq', grad_mixed.astype(jnp.float32), mixed.astype(jnp.float32))
    grad_value = jnp.einsum('hqk,qhd->khd', probs.astype(jnp.bfloat16).astype(jnp.float32), grad_mixed.astype(jnp.float32))
    grad_probs = jnp.einsum('qhd,khd->hqk', grad_mixed.astype(jnp.float32), value.astype(jnp.float32))
    grad_scores = (probs * (grad_probs - delta[:, :, None]) * SCALE).astype(jnp.bfloat16).astype(jnp.float32)
    grad_query = jnp.einsum('hqk,khd->qhd', grad_scores, key.astype(jnp.float32))
    grad_key = jnp.einsum('hqk,qhd->khd', grad_scores, query.astype(jnp.float32))
    return (grad_query, grad_key, grad_value)

def layer_forward(state, allowed, cosine, sine, params):
    gain1, bias1, gain2, bias2, w_qkv, b_qkv, w_up, b_up, w_out, b_out, w_down, b_down = params
    mean = lax.optimization_barrier(jnp.mean(state, axis=1, keepdims=True))
    spread = lax.optimization_barrier(jnp.mean(state * state, axis=1, keepdims=True)) - mean * mean
    inverse = lax.rsqrt(spread + EPS)
    normed = (state - mean) * inverse
    first = (normed * gain1 + bias1).astype(jnp.bfloat16)
    second = (normed * gain2 + bias2).astype(jnp.bfloat16)
    qkv = (jnp.dot(first, w_qkv, preferred_element_type=jnp.float32) + b_qkv).reshape(-1, H, 3, HD)
    query = rotate(qkv[:, :, 0], cosine, sine).astype(jnp.bfloat16)
    key = rotate(qkv[:, :, 1], cosine, sine).astype(jnp.bfloat16)
    value = qkv[:, :, 2].astype(jnp.bfloat16)
    mixed, lse = attend(query, key, value, allowed)
    up = jnp.dot(second, w_up, preferred_element_type=jnp.float32) + b_up
    act = gelu_exact(up).astype(jnp.bfloat16)
    flat = mixed.reshape(-1, D)
    branches = jnp.dot(flat, w_out, preferred_element_type=jnp.float32) + jnp.dot(act, w_down, preferred_element_type=jnp.float32)
    result = state + branches + b_out + b_down
    return (result, (normed, inverse, first, second, query, key, value, mixed, lse, up, act))

def layer_backward(grad, allowed, cosine, sine, params, cache):
    gain1, bias1, gain2, bias2, w_qkv, b_qkv, w_up, b_up, w_out, b_out, w_down, b_down = params
    normed, inverse, first, second, query, key, value, mixed, lse, up, act = cache
    grad_b = grad.astype(jnp.bfloat16)
    flat = mixed.reshape(-1, D)
    g_wout = jnp.dot(flat.T, grad_b, preferred_element_type=jnp.float32)
    g_wdown = jnp.dot(act.T, grad_b, preferred_element_type=jnp.float32)
    g_bout = lax.optimization_barrier(jnp.sum(grad, axis=0))
    grad_mixed = jnp.dot(grad_b, w_out.T, preferred_element_type=jnp.float32).astype(jnp.bfloat16).reshape(-1, H, HD)
    grad_act = jnp.dot(grad_b, w_down.T, preferred_element_type=jnp.float32)
    grad_up = grad_act * gelu_slope(up)
    g_bup = lax.optimization_barrier(jnp.sum(grad_up, axis=0))
    grad_up_b = grad_up.astype(jnp.bfloat16)
    grad_query, grad_key, grad_value = attend_back(query, key, value, mixed, grad_mixed, lse, allowed)
    grad_query = unrotate(grad_query, cosine, sine)
    grad_key = unrotate(grad_key, cosine, sine)
    grad_qkv = jnp.stack([grad_query, grad_key, grad_value], axis=2).reshape(-1, 3 * D)
    g_bqkv = lax.optimization_barrier(jnp.sum(grad_qkv, axis=0))
    grad_qkv_b = grad_qkv.astype(jnp.bfloat16)
    g_wqkv = jnp.dot(first.T, grad_qkv_b, preferred_element_type=jnp.float32)
    g_wup = jnp.dot(second.T, grad_up_b, preferred_element_type=jnp.float32)
    grad_first = jnp.dot(grad_qkv_b, w_qkv.T, preferred_element_type=jnp.float32)
    grad_second = jnp.dot(grad_up_b, w_up.T, preferred_element_type=jnp.float32)
    g_gain1 = lax.optimization_barrier(jnp.sum(grad_first * normed, axis=0))
    g_bias1 = lax.optimization_barrier(jnp.sum(grad_first, axis=0))
    g_gain2 = lax.optimization_barrier(jnp.sum(grad_second * normed, axis=0))
    g_bias2 = lax.optimization_barrier(jnp.sum(grad_second, axis=0))
    grad_norm = grad_first * gain1 + grad_second * gain2
    centred = grad_norm - lax.optimization_barrier(jnp.mean(grad_norm, axis=1, keepdims=True)) - normed * lax.optimization_barrier(jnp.mean(grad_norm * normed, axis=1, keepdims=True))
    grad_x = grad + inverse * centred
    grads = (g_gain1, g_bias1, g_gain2, g_bias2, g_wqkv, g_bqkv, g_wup, g_bup, g_wout, g_bout, g_wdown, g_bout)
    return (grad_x, grads)

def reference(x_in, cotangent, segment_ids, norm1_gain, norm1_bias, norm2_gain, norm2_bias, w_qkv, b_qkv, w_up, b_up, w_out, b_out, w_down, b_down):
    stacked = (norm1_gain, norm1_bias, norm2_gain, norm2_bias, w_qkv, b_qkv, w_up, b_up, w_out, b_out, w_down, b_down)
    cosine, sine = rope_tables(SEQ)
    places = jnp.arange(SEQ, dtype=jnp.int32)
    causal = places[:, None] >= places[None, :]

    def group(totals, item):
        state, grad, seg = item
        allowed = causal & (seg[:, None] == seg[None, :])
        caches = []
        for layer in range(LAYERS):
            params = tuple((p[layer] for p in stacked))
            state, cache = layer_forward(state, allowed, cosine, sine, params)
            caches.append(cache)
        per_layer = [None] * LAYERS
        for layer in reversed(range(LAYERS)):
            params = tuple((p[layer] for p in stacked))
            grad, grads = layer_backward(grad, allowed, cosine, sine, params, caches[layer])
            per_layer[layer] = grads
        joined = tuple((jnp.stack([g[index] for g in per_layer]) for index in range(12)))
        totals = tuple((a + b for a, b in zip(totals, joined)))
        return (totals, (state, grad))
    zeros = tuple((jnp.zeros(p.shape, jnp.float32) for p in stacked))
    items = (x_in.reshape(SEQS, SEQ, D), cotangent.reshape(SEQS, SEQ, D), segment_ids)
    totals, (outputs, grads_in) = lax.scan(group, zeros, items)
    return (outputs.reshape(TOKENS, D), grads_in.reshape(TOKENS, D), totals[0], totals[1], totals[2], totals[3], totals[4], totals[5], totals[6], totals[7], totals[8], totals[9], totals[10], totals[11])
```

```python
import jax
import jax.numpy as jnp
from jax import lax
from jax.experimental import pallas as pl
from jax.experimental.pallas import tpu as pltpu
from jax.sharding import PartitionSpec as P

D = 768
HD = 64
ROT = 16
LAYERS = 2


EPS = 1e-05
NEG = -1e30
SCALE = 0.125
INV_ROOT2 = 0.7071067811865476
INV_ROOT_TWO_PI = 0.3989422804014327


def rope_tables(length):
    half = ROT // 2
    freq = 10000.0 ** (-(jnp.arange(half, dtype=jnp.float32) * 2.0) / ROT)
    angle = jnp.arange(length, dtype=jnp.float32)[:, None] * freq[None, :]
    cosine = jnp.concatenate([jnp.cos(angle), jnp.cos(angle)], axis=1)
    sine = jnp.concatenate([jnp.sin(angle), jnp.sin(angle)], axis=1)
    return (cosine, sine)


def rotate(values, cosine, sine):
    part = values[..., :ROT]
    lower = part[..., : ROT // 2]
    upper = part[..., ROT // 2 :]
    turned = jnp.concatenate([-upper, lower], axis=-1)
    moved = part * cosine[:, None, :] + turned * sine[:, None, :]
    return jnp.concatenate([moved, values[..., ROT:]], axis=-1)


def unrotate(grads, cosine, sine):
    part = grads[..., :ROT]
    lower = part[..., : ROT // 2]
    upper = part[..., ROT // 2 :]
    turned = jnp.concatenate([upper, -lower], axis=-1)
    moved = part * cosine[:, None, :] + turned * sine[:, None, :]
    return jnp.concatenate([moved, grads[..., ROT:]], axis=-1)


def gelu_exact(values):
    return 0.5 * values * (1.0 + jax.scipy.special.erf(values * INV_ROOT2))


def gelu_slope(values):
    return (
        0.5 * (1.0 + jax.scipy.special.erf(values * INV_ROOT2))
        + values * jnp.exp(-0.5 * values * values) * INV_ROOT_TWO_PI
    )


BF = jnp.bfloat16
F32 = jnp.float32
MESH_ID = pl.DeviceIdType.MESH
PIECES = 4


def greet():
    row = 1 - lax.axis_index("row")
    col = 1 - lax.axis_index("col")
    barrier = pltpu.get_barrier_semaphore()
    pl.semaphore_signal(barrier, inc=1, device_id={"row": row}, device_id_type=MESH_ID)
    pl.semaphore_signal(barrier, inc=1, device_id={"col": col}, device_id_type=MESH_ID)
    pl.semaphore_wait(barrier, 2)
    return row, col


def reduce_body(*refs):
    if len(refs) == 7:
        part, out, got_row, mine, got_col, send, recv = refs
        extra = None
    else:
        part, extra, out, extra_out, got_row, mine, got_col, pair, got_extra, send, recv = refs
    half = mine.shape[0]
    piece = half // PIECES
    row, col = greet()
    own = (1 - row) * half
    theirs = row * half
    first, second, third = [], [], []
    for k in range(PIECES):
        at = pl.multiple_of(theirs + k * piece, piece)
        copy = pltpu.make_async_remote_copy(
            part.at[pl.ds(at, piece)], got_row.at[pl.ds(k * piece, piece)],
            send.at[0, k], recv.at[0, k], device_id={"row": row}, device_id_type=MESH_ID)
        copy.start()
        first.append(copy)
    if extra is not None:
        over_row = pltpu.make_async_remote_copy(
            extra, got_extra.at[0], send.at[3, 0], recv.at[3, 0],
            device_id={"row": row}, device_id_type=MESH_ID)
        over_row.start()
    for k in range(PIECES):
        here = pl.ds(k * piece, piece)
        at = pl.multiple_of(own + k * piece, piece)
        first[k].wait_recv()
        mine[here, :] = (part[pl.ds(at, piece), :] + got_row[here, :]).astype(BF)
        copy = pltpu.make_async_remote_copy(
            mine.at[here], got_col.at[here], send.at[1, k], recv.at[1, k],
            device_id={"col": col}, device_id_type=MESH_ID)
        copy.start()
        second.append(copy)
    if extra is not None:
        over_row.wait_recv()
        pair[...] = extra[...] + got_extra[0]
        over_col = pltpu.make_async_remote_copy(
            pair, got_extra.at[1], send.at[3, 1], recv.at[3, 1],
            device_id={"col": col}, device_id_type=MESH_ID)
        over_col.start()
    for k in range(PIECES):
        here = pl.ds(k * piece, piece)
        at = pl.multiple_of(own + k * piece, piece)
        second[k].wait_recv()
        out[pl.ds(at, piece), :] = mine[here, :].astype(F32) + got_col[here, :].astype(F32)
        copy = pltpu.make_async_remote_copy(
            out.at[pl.ds(at, piece)], out.at[pl.ds(at, piece)], send.at[2, k], recv.at[2, k],
            device_id={"row": row}, device_id_type=MESH_ID)
        copy.start()
        third.append(copy)
    if extra is not None:
        over_col.wait_recv()
        extra_out[...] = pair[...] + got_extra[1]
        over_row.wait_send()
        over_col.wait_send()
    for k in range(PIECES):
        third[k].wait_recv()
        for copy in (first[k], second[k], third[k]):
            copy.wait_send()


def group_sum(part, extra=None):
    rows, width = part.shape
    half = rows // lax.axis_size("row")
    vmem = pl.BlockSpec(memory_space=pltpu.VMEM)
    out_shape = [jax.ShapeDtypeStruct((rows, width), F32)]
    scratch = [pltpu.VMEM((half, width), F32), pltpu.VMEM((half, width), BF),
               pltpu.VMEM((half, width), BF)]
    args = [part]
    if extra is not None:
        args.append(extra)
        out_shape.append(jax.ShapeDtypeStruct(extra.shape, F32))
        scratch += [pltpu.VMEM(extra.shape, F32), pltpu.VMEM((2,) + extra.shape, F32)]
    result = pl.pallas_call(
        reduce_body,
        out_shape=out_shape,
        in_specs=[vmem] * len(args),
        out_specs=[vmem] * len(out_shape),
        scratch_shapes=scratch + [
            pltpu.SemaphoreType.DMA((4, PIECES)), pltpu.SemaphoreType.DMA((4, PIECES))],
        compiler_params=pltpu.CompilerParams(
            collective_id=0 if extra is None else 2, has_side_effects=True),
        name="group_sum",
    )(*args)
    return result[0] if extra is None else result


def gather_body(x, cot, vec, x_out, cot_out, vec_out, send, recv):
    half, width = x.shape
    row, col = greet()
    my_rows = pl.ds(pl.multiple_of((1 - row) * half, half), half)
    my_cols = pl.ds(pl.multiple_of((1 - col) * width, width), width)
    their_cols = pl.ds(pl.multiple_of(col * width, width), width)
    every = pl.ds(0, vec.shape[0])
    jobs = [(x, x_out, my_rows), (vec, vec_out, every), (cot, cot_out, my_rows)]
    copies = []
    first = []
    for k, (own, out, rows) in enumerate(jobs):
        copy = pltpu.make_async_remote_copy(
            own, out.at[rows, my_cols], send.at[0, k], recv.at[0, k],
            device_id={"col": col}, device_id_type=MESH_ID)
        copy.start()
        first.append(copy)
    for k, (own, out, rows) in enumerate(jobs):
        if rows is my_rows:
            copy = pltpu.make_async_remote_copy(
                own, out.at[rows, my_cols], send.at[1, k], recv.at[1, k],
                device_id={"row": row}, device_id_type=MESH_ID)
            copy.start()
            copies.append(copy)
    for own, out, rows in jobs:
        out[rows, my_cols] = own[...]
    for k, (own, out, rows) in enumerate(jobs):
        first[k].wait_recv()
        if rows is my_rows:
            copy = pltpu.make_async_remote_copy(
                out.at[rows, their_cols], out.at[rows, their_cols], send.at[2, k], recv.at[2, k],
                device_id={"row": row}, device_id_type=MESH_ID)
            copy.start()
            copies.append(copy)
    for copy in copies:
        copy.wait_recv()
    for copy in first + copies:
        copy.wait_send()


def group_gather(x, cot, vec):
    half, width = x.shape
    rows, wide = half * lax.axis_size("row"), width * lax.axis_size("col")
    vmem = pl.BlockSpec(memory_space=pltpu.VMEM)
    return pl.pallas_call(
        gather_body,
        out_shape=[
            jax.ShapeDtypeStruct((rows, wide), x.dtype),
            jax.ShapeDtypeStruct((rows, wide), cot.dtype),
            jax.ShapeDtypeStruct((vec.shape[0], wide), vec.dtype),
        ],
        in_specs=[vmem] * 3,
        out_specs=[vmem] * 3,
        scratch_shapes=[pltpu.SemaphoreType.DMA((3, 3)), pltpu.SemaphoreType.DMA((3, 3))],
        compiler_params=pltpu.CompilerParams(collective_id=1, has_side_effects=True),
        name="group_gather",
    )(x, cot, vec)


def ring_body(n, per, q_in, m_in, q_out, m_out, q_got, m_got, q_swap, m_swap, send, recv, swap_send, swap_recv):
    layers = q_in.shape[0]
    cut = m_in.shape[2] // 2
    here = lax.axis_index("dp")
    odd = lax.rem(here, 2)
    pos = here // 2 + odd * (n - 1 - 2 * (here // 2))
    mine = lax.axis_index("col")
    other = 1 - mine

    def device(place):
        late = place // (n // 2)
        return 2 * (place + late * (n - 1 - 2 * place)) + late

    nexts = device(lax.rem(pos + 1, n))
    prevs = device(lax.rem(pos + n - 1, n))
    targets = (nexts, prevs)
    barrier = pltpu.get_barrier_semaphore()
    pl.semaphore_signal(barrier, inc=1, device_id={"dp": nexts}, device_id_type=MESH_ID)
    pl.semaphore_signal(barrier, inc=1, device_id={"dp": prevs}, device_id_type=MESH_ID)
    pl.semaphore_signal(barrier, inc=1, device_id={"col": other}, device_id_type=MESH_ID)
    pl.semaphore_wait(barrier, 3)

    def chunk(d, back):
        sign = 1 if d % 2 == 0 else -1
        return lax.rem(pos - sign * back + 2 * n, n)

    def view(q, m, p):
        return q if p == 0 else m.at[pl.ds((p - 1) * cut, cut)]

    started = []

    def go(src, dst, d, p, step):
        copy = pltpu.make_async_remote_copy(
            src, dst, send.at[d, p, step], recv.at[d, p, step],
            device_id={"dp": targets[d % 2]}, device_id_type=MESH_ID)
        copy.start()
        started.append(copy)
        return copy

    flight = {}
    for p in range(3):
        for d in range(layers):
            at = chunk(d, 0)
            flight[d, p] = go(
                view(q_in.at[d, at], m_in.at[d, at], p),
                view(q_got.at[d, 0], m_got.at[d, 0], p), d, p, 0)
    for step in range(n - 1):
        for p in range(3):
            for d in range(layers):
                flight[d, p].wait_recv()
                own = chunk(d, step + 1)
                if p == 0:
                    q_got[d, step] = (q_got[d, step].astype(F32) + q_in[d, own].astype(F32)).astype(BF)
                else:
                    rows = pl.ds((p - 1) * cut, cut)
                    m_got[d, step, rows] = (
                        m_got[d, step, rows].astype(F32) + m_in[d, own, rows].astype(F32)).astype(BF)
                if step < n - 2:
                    flight[d, p] = go(
                        view(q_got.at[d, step], m_got.at[d, step], p),
                        view(q_got.at[d, step + 1], m_got.at[d, step + 1], p), d, p, step + 1)
    last = n - 2
    swaps = []
    for d in range(layers):
        rows = pl.ds(pl.multiple_of(other * per, per), per)
        one = pltpu.make_async_remote_copy(
            q_got.at[d, last, other], q_swap.at[d], swap_send.at[d, 0], swap_recv.at[d, 0],
            device_id={"col": other}, device_id_type=MESH_ID)
        two = pltpu.make_async_remote_copy(
            m_got.at[d, last, rows], m_swap.at[d], swap_send.at[d, 1], swap_recv.at[d, 1],
            device_id={"col": other}, device_id_type=MESH_ID)
        one.start()
        two.start()
        swaps.append((one, two))
    mine_rows = pl.ds(pl.multiple_of(mine * per, per), per)
    other_rows = pl.ds(pl.multiple_of(other * per, per), per)
    rest = pl.ds(2 * per, m_in.shape[2] - 2 * per)
    for d in range(layers):
        at = chunk(d, n - 1)
        q_out[d, at, mine] = q_got[d, last, mine]
        m_out[d, at, mine_rows] = m_got[d, last, mine_rows]
        m_out[d, at, rest] = m_got[d, last, rest]
    for d in range(layers):
        at = chunk(d, n - 1)
        swaps[d][0].wait_recv()
        q_out[d, at, other] = q_swap[d]
        swaps[d][1].wait_recv()
        m_out[d, at, other_rows] = m_swap[d]
    for p in range(3):
        for d in range(layers):
            at = chunk(d, n - 1)
            spot = view(q_out.at[d, at], m_out.at[d, at], p)
            flight[d, p] = go(spot, spot, d, p, n - 1)
    for step in range(n - 1):
        for p in range(3):
            for d in range(layers):
                flight[d, p].wait_recv()
                if step < n - 2:
                    at = chunk(d, step)
                    spot = view(q_out.at[d, at], m_out.at[d, at], p)
                    flight[d, p] = go(spot, spot, d, p, n + step)
    for pair in swaps:
        for copy in pair:
            copy.wait_send()
    for copy in started:
        copy.wait_send()


def ring_sum(q, m):
    layers, n, _, per, width = q.shape
    vmem = pl.BlockSpec(memory_space=pltpu.VMEM)
    return pl.pallas_call(
        lambda *refs: ring_body(n, per, *refs),
        out_shape=[jax.ShapeDtypeStruct(q.shape, BF), jax.ShapeDtypeStruct(m.shape, BF)],
        in_specs=[vmem] * 2,
        out_specs=[vmem] * 2,
        scratch_shapes=[
            pltpu.VMEM((layers, n - 1) + q.shape[2:], BF),
            pltpu.VMEM((layers, n - 1) + m.shape[2:], BF),
            pltpu.VMEM((layers, per, width), BF),
            pltpu.VMEM((layers, per, m.shape[3]), BF),
            pltpu.SemaphoreType.DMA((layers, 3, 2 * n)),
            pltpu.SemaphoreType.DMA((layers, 3, 2 * n)),
            pltpu.SemaphoreType.DMA((layers, 2)),
            pltpu.SemaphoreType.DMA((layers, 2)),
        ],
        compiler_params=pltpu.CompilerParams(
            collective_id=3, has_side_effects=True, vmem_limit_bytes=60 * 1024 * 1024),
        name="ring_sum",
    )(q, m)


def make_scores(query, key, allowed):
    scores = jnp.einsum("hqd,hkd->hqk", query, key, preferred_element_type=F32) * SCALE
    return jnp.where(allowed[None], scores, NEG)


def swap_col(value):
    return lax.ppermute(value, "col", [(0, 1), (1, 0)])


def columns_whole(own):
    col = lax.axis_index("col")
    depth, width = own.shape[1], own.shape[2] // 2
    got = swap_col(lax.dynamic_slice_in_dim(own, (1 - col) * width, width, 2))
    kept = lax.dynamic_slice_in_dim(own, col * width, width, 2)
    low = jnp.where(col == 0, kept, got)
    high = jnp.where(col == 0, got, kept)
    return jnp.concatenate([low, high], axis=1)


def rows_whole(grad):
    col = lax.axis_index("col")
    depth = grad.shape[0] // 2
    got = swap_col(lax.dynamic_slice_in_dim(grad, (1 - col) * depth, depth, 0))
    kept = lax.dynamic_slice_in_dim(grad, col * depth, depth, 0)
    low = jnp.where(col == 0, kept, got)
    high = jnp.where(col == 0, got, kept)
    return jnp.concatenate([low, high], axis=1)


def forward_layer(state, allowed, cosine, sine, params):
    gain1, bias1, gain2, bias2, w_qkv, b_qkv, w_up, b_up, w_out, w_down, b_both = params
    width = state.shape[1]
    mean = jnp.sum(state, axis=1, keepdims=True) / width
    squares = jnp.sum(state * state, axis=1, keepdims=True) / width
    inverse = lax.rsqrt(squares - mean * mean + EPS)
    normed = (state - mean) * inverse
    first = (normed * gain1 + bias1).astype(BF)
    second = (normed * gain2 + bias2).astype(BF)
    rows = state.shape[0]
    qkv = (jnp.dot(first, w_qkv, preferred_element_type=F32) + b_qkv).reshape(rows, -1, 3, HD)
    query = rotate(qkv[:, :, 0], cosine, sine).astype(BF).transpose(1, 0, 2)
    key = rotate(qkv[:, :, 1], cosine, sine).astype(BF).transpose(1, 0, 2)
    value = qkv[:, :, 2].astype(BF).transpose(1, 0, 2)
    scores = make_scores(query, key, allowed)
    top = jnp.max(scores, axis=-1, keepdims=True)
    lse = top + jnp.log(jnp.sum(jnp.exp(scores - top), axis=-1, keepdims=True))
    probs = jnp.exp(scores - lse).astype(BF)
    mixed = jnp.einsum("hqk,hkd->qhd", probs, value, preferred_element_type=F32)
    mixed = mixed.astype(BF).reshape(rows, -1)
    up = jnp.dot(second, w_up, preferred_element_type=F32) + b_up
    act = gelu_exact(up).astype(BF)
    part = jnp.dot(mixed, w_out, preferred_element_type=F32) + jnp.dot(
        act, w_down, preferred_element_type=F32)
    result = state + group_sum(part) + b_both
    return result, (normed, inverse, first, second, query, key, value, mixed, lse, up, act)


def backward_layer(grad, allowed, cosine, sine, params, cache):
    gain1, bias1, gain2, bias2, w_qkv, b_qkv, w_up, b_up, w_out, w_down, b_both = params
    normed, inverse, first, second, query, key, value, mixed, lse, up, act = cache
    rows, width = grad.shape
    grad_b = grad.astype(BF)
    g_bout = jnp.sum(grad, axis=0)
    grad_mixed = jnp.einsum("td,kd->tk", grad_b, w_out, preferred_element_type=F32).astype(BF)
    grad_act = jnp.einsum("td,kd->tk", grad_b, w_down, preferred_element_type=F32)
    grad_up = grad_act * gelu_slope(up)
    g_bup = jnp.sum(grad_up, axis=0)
    grad_up_b = grad_up.astype(BF)
    scores = make_scores(query, key, allowed)
    probs = jnp.exp(scores - lse)
    grad_heads = grad_mixed.reshape(rows, -1, HD).transpose(1, 0, 2)
    mixed_heads = mixed.reshape(rows, -1, HD).transpose(1, 0, 2)
    delta = jnp.sum(grad_heads.astype(F32) * mixed_heads.astype(F32), axis=-1, keepdims=True)
    grad_value = jnp.einsum("hqk,hqd->khd", probs.astype(BF), grad_heads, preferred_element_type=F32)
    grad_probs = jnp.einsum("hqd,hkd->hqk", grad_heads, value, preferred_element_type=F32)
    grad_scores = (probs * (grad_probs - delta) * SCALE).astype(BF)
    grad_query = jnp.einsum("hqk,hkd->qhd", grad_scores, key, preferred_element_type=F32)
    grad_key = jnp.einsum("hqk,hqd->khd", grad_scores, query, preferred_element_type=F32)
    grad_query = unrotate(grad_query, cosine, sine)
    grad_key = unrotate(grad_key, cosine, sine)
    grad_qkv = jnp.stack([grad_query, grad_key, grad_value], axis=2).reshape(rows, -1)
    g_bqkv = jnp.sum(grad_qkv, axis=0)
    grad_qkv_b = grad_qkv.astype(BF)
    part_first = jnp.einsum("tn,dn->td", grad_qkv_b, w_qkv, preferred_element_type=F32)
    part_second = jnp.einsum("tn,dn->td", grad_up_b, w_up, preferred_element_type=F32)
    part = part_first * gain1 + part_second * gain2
    g_wout = jnp.einsum("tk,td->kd", mixed, grad_b, preferred_element_type=F32)
    g_wdown = jnp.einsum("tk,td->kd", act, grad_b, preferred_element_type=F32)
    g_wqkv = jnp.einsum("td,tn->dn", first, grad_qkv_b, preferred_element_type=F32)
    g_wup = jnp.einsum("td,tn->dn", second, grad_up_b, preferred_element_type=F32)
    shares = lax.axis_size("row") * lax.axis_size("col")
    narrow = jnp.concatenate([
        jnp.stack([
            jnp.sum(part_first * normed, axis=0), jnp.sum(part_first, axis=0),
            jnp.sum(part_second * normed, axis=0), jnp.sum(part_second, axis=0),
            g_bout / shares,
        ]),
        jnp.zeros((3, width), F32),
    ])
    grad_norm, narrow = group_sum(part, narrow)
    centred = (
        grad_norm
        - jnp.sum(grad_norm, axis=1, keepdims=True) / width
        - normed * (jnp.sum(grad_norm * normed, axis=1, keepdims=True) / width)
    )
    grad_x = grad + inverse * centred
    heavy = (g_wqkv.astype(BF), g_wup.astype(BF), g_wout.astype(BF), g_wdown.astype(BF))
    return grad_x, heavy, (g_bqkv, g_bup), narrow


def per_device(
    x_in, cotangent, segment_ids, norm1_gain, norm1_bias, norm2_gain, norm2_bias,
    w_qkv, b_qkv, w_up, b_up, w_out, b_out, w_down, b_down,
):
    half, part_width = x_in.shape
    row = lax.axis_index("row")
    col = lax.axis_index("col")
    length = segment_ids.shape[1]
    layers = w_qkv.shape[0]
    cosine, sine = rope_tables(length)
    places = jnp.arange(length, dtype=jnp.int32)
    labels = segment_ids[0]
    allowed = (places[:, None] >= places[None, :]) & (labels[:, None] == labels[None, :])
    vec = jnp.stack([norm1_gain, norm1_bias, norm2_gain, norm2_bias, b_out + b_down])
    vec = vec.reshape(-1, part_width)
    pad = -vec.shape[0] % 8
    state_in, cot, vec = group_gather(x_in, cotangent.astype(BF), jnp.pad(vec, ((0, pad), (0, 0))))
    grad_in = cot.astype(F32)
    vectors = vec[: vec.shape[0] - pad].reshape(5, layers, -1)
    wide_qkv, wide_up, gate = [], [], vec
    for l in range(layers):
        gate, block = lax.optimization_barrier((gate, w_qkv[l : l + 1]))
        wide_qkv.append(columns_whole(block)[0])
        gate, block = lax.optimization_barrier((gate, w_up[l : l + 1]))
        wide_up.append(columns_whole(block)[0])
        gate = wide_up[-1]

    def own(whole):
        return lax.dynamic_slice(whole, (row * half, col * part_width), (half, part_width))

    params = [
        (vectors[0, l], vectors[1, l], vectors[2, l], vectors[3, l], wide_qkv[l], b_qkv[l],
         wide_up[l], b_up[l], w_out[l], w_down[l], vectors[4, l])
        for l in range(layers)
    ]
    state = state_in
    caches = []
    for layer in range(layers):
        state, cache = forward_layer(state, allowed, cosine, sine, params[layer])
        caches.append(cache)
    y_out = x_in + own(state - state_in)
    grad = grad_in
    heavy = [None] * layers
    thin = [None] * layers
    narrow = [None] * layers
    for layer in reversed(range(layers)):
        grad, heavy[layer], thin[layer], narrow[layer] = backward_layer(
            grad, allowed, cosine, sine, params[layer], caches[layer])
    x_grad = cotangent + own(grad - grad_in)
    n = lax.axis_size("dp")
    width = state.shape[1]
    per = width // 2 // n
    if per % 16 == 0 and (w_out.shape[1] // n) % 8 == 0 and layers == 2:
        q = jnp.stack([h[0].reshape(2, n, per, -1).transpose(1, 0, 2, 3) for h in heavy])
        blocks = []
        for layer in range(layers):
            g_bqkv, g_bup = thin[layer]
            g_bqkv = jnp.pad(g_bqkv, (0, width - g_bqkv.shape[0]))
            small = jnp.concatenate([narrow[layer][:5], g_bqkv[None], g_bup.reshape(-1, width)])
            small = jnp.pad(small, ((0, 8 - small.shape[0]), (0, 0))).astype(BF)
            small = jnp.pad(small[None], ((0, n - 1), (0, 0), (0, 0)))
            _, b, c, d = heavy[layer]
            blocks.append(jnp.concatenate([
                b.reshape(2, n, per, -1).transpose(1, 0, 2, 3).reshape(n, 2 * per, -1),
                d.reshape(n, -1, width), c.reshape(n, -1, width), small], axis=1))
        q, m = ring_sum(q, jnp.stack(blocks))
        deep = w_down.shape[1] // n
        flat = w_out.shape[1] // n
        g_wqkv = q.transpose(0, 1, 3, 2, 4).reshape(w_qkv.shape).astype(F32)
        g_wup = m[:, :, : 2 * per].reshape(layers, n, 2, per, -1).transpose(0, 1, 3, 2, 4)
        g_wup = g_wup.reshape(w_up.shape).astype(F32)
        g_wdown = m[:, :, 2 * per : 2 * per + deep].reshape(w_down.shape).astype(F32)
        g_wout = m[:, :, 2 * per + deep : 2 * per + deep + flat].reshape(w_out.shape).astype(F32)
        small = m[:, 0, 2 * per + deep + flat :].astype(F32)
        narrow = small[:, :5]
        g_bqkv = small[:, 5, : b_qkv.shape[1]]
        g_bup = small[:, 6].reshape(b_up.shape)
    else:
        summed = []
        for layer in range(layers):
            a, b, c, d = heavy[layer]
            summed.append(lax.psum((rows_whole(a), rows_whole(b), c, d), "dp"))
        g_bqkv, g_bup, narrow = lax.psum((
            jnp.stack([t[0] for t in thin]), jnp.stack([t[1] for t in thin]),
            jnp.stack([t[:5] for t in narrow])), "dp")
        g_wqkv, g_wup, g_wout, g_wdown = (
            jnp.stack([h[k] for h in summed]).astype(F32) for k in range(4))
    narrow = lax.dynamic_slice_in_dim(narrow, col * part_width, part_width, 2)
    g_bout = narrow[:, 4]
    return (
        y_out, x_grad, narrow[:, 0], narrow[:, 1], narrow[:, 2], narrow[:, 3],
        g_wqkv, g_bqkv, g_wup, g_bup, g_wout, g_bout, g_wdown, g_bout,
    )


def solution(mesh):
    in_specs = (
        P(("dp", "row"), "col"),
        P(("dp", "row"), "col"),
        P("dp", None),
        P(None, "col"),
        P(None, "col"),
        P(None, "col"),
        P(None, "col"),
        P(None, "col", "row"),
        P(None, ("row", "col")),
        P(None, "col", "row"),
        P(None, ("row", "col")),
        P(None, ("row", "col"), None),
        P(None, "col"),
        P(None, ("row", "col"), None),
        P(None, "col"),
    )
    out_specs = (
        P(("dp", "row"), "col"),
        P(("dp", "row"), "col"),
        P(None, "col"),
        P(None, "col"),
        P(None, "col"),
        P(None, "col"),
        P(None, "col", "row"),
        P(None, ("row", "col")),
        P(None, "col", "row"),
        P(None, ("row", "col")),
        P(None, ("row", "col"), None),
        P(None, "col"),
        P(None, ("row", "col"), None),
        P(None, "col"),
    )
    return jax.shard_map(
        per_device, mesh=mesh, in_specs=in_specs, out_specs=out_specs, check_vma=False
    )
```

```python
import jax
import jax.numpy as jnp
from jax import lax
from jax.experimental import pallas as pl
from jax.experimental.pallas import tpu as pltpu
from jax.sharding import PartitionSpec as P

D = 768
HD = 64
ROT = 16
LAYERS = 2


EPS = 1e-05
NEG = -1e30
SCALE = 0.125
INV_ROOT2 = 0.7071067811865476
INV_ROOT_TWO_PI = 0.3989422804014327


def rope_tables(length):
    half = ROT // 2
    freq = 10000.0 ** (-(jnp.arange(half, dtype=jnp.float32) * 2.0) / ROT)
    angle = jnp.arange(length, dtype=jnp.float32)[:, None] * freq[None, :]
    cosine = jnp.concatenate([jnp.cos(angle), jnp.cos(angle)], axis=1)
    sine = jnp.concatenate([jnp.sin(angle), jnp.sin(angle)], axis=1)
    return (cosine, sine)


def rotate(values, cosine, sine):
    part = values[..., :ROT]
    lower = part[..., : ROT // 2]
    upper = part[..., ROT // 2 :]
    turned = jnp.concatenate([-upper, lower], axis=-1)
    moved = part * cosine[:, None, :] + turned * sine[:, None, :]
    return jnp.concatenate([moved, values[..., ROT:]], axis=-1)


def unrotate(grads, cosine, sine):
    part = grads[..., :ROT]
    lower = part[..., : ROT // 2]
    upper = part[..., ROT // 2 :]
    turned = jnp.concatenate([upper, -lower], axis=-1)
    moved = part * cosine[:, None, :] + turned * sine[:, None, :]
    return jnp.concatenate([moved, grads[..., ROT:]], axis=-1)


def gelu_exact(values):
    return 0.5 * values * (1.0 + jax.scipy.special.erf(values * INV_ROOT2))


def gelu_slope(values):
    return (
        0.5 * (1.0 + jax.scipy.special.erf(values * INV_ROOT2))
        + values * jnp.exp(-0.5 * values * values) * INV_ROOT_TWO_PI
    )


BF = jnp.bfloat16
F32 = jnp.float32
MESH_ID = pl.DeviceIdType.MESH
PIECES = 4


def greet():
    row = 1 - lax.axis_index("row")
    col = 1 - lax.axis_index("col")
    barrier = pltpu.get_barrier_semaphore()
    pl.semaphore_signal(barrier, inc=1, device_id={"row": row}, device_id_type=MESH_ID)
    pl.semaphore_signal(barrier, inc=1, device_id={"col": col}, device_id_type=MESH_ID)
    pl.semaphore_wait(barrier, 2)
    return row, col


def reduce_body(*refs):
    if len(refs) == 7:
        part, out, got_row, mine, got_col, send, recv = refs
        extra = None
    else:
        part, extra, out, extra_out, got_row, mine, got_col, pair, got_extra, send, recv = refs
    half = mine.shape[0]
    piece = half // PIECES
    row, col = greet()
    own = (1 - row) * half
    theirs = row * half
    first, second, third = [], [], []
    for k in range(PIECES):
        at = pl.multiple_of(theirs + k * piece, piece)
        copy = pltpu.make_async_remote_copy(
            part.at[pl.ds(at, piece)], got_row.at[pl.ds(k * piece, piece)],
            send.at[0, k], recv.at[0, k], device_id={"row": row}, device_id_type=MESH_ID)
        copy.start()
        first.append(copy)
    if extra is not None:
        over_row = pltpu.make_async_remote_copy(
            extra, got_extra.at[0], send.at[3, 0], recv.at[3, 0],
            device_id={"row": row}, device_id_type=MESH_ID)
        over_row.start()
    for k in range(PIECES):
        here = pl.ds(k * piece, piece)
        at = pl.multiple_of(own + k * piece, piece)
        first[k].wait_recv()
        mine[here, :] = (part[pl.ds(at, piece), :] + got_row[here, :]).astype(BF)
        copy = pltpu.make_async_remote_copy(
            mine.at[here], got_col.at[here], send.at[1, k], recv.at[1, k],
            device_id={"col": col}, device_id_type=MESH_ID)
        copy.start()
        second.append(copy)
    if extra is not None:
        over_row.wait_recv()
        pair[...] = extra[...] + got_extra[0]
        over_col = pltpu.make_async_remote_copy(
            pair, got_extra.at[1], send.at[3, 1], recv.at[3, 1],
            device_id={"col": col}, device_id_type=MESH_ID)
        over_col.start()
    for k in range(PIECES):
        here = pl.ds(k * piece, piece)
        at = pl.multiple_of(own + k * piece, piece)
        second[k].wait_recv()
        out[pl.ds(at, piece), :] = mine[here, :].astype(F32) + got_col[here, :].astype(F32)
        copy = pltpu.make_async_remote_copy(
            out.at[pl.ds(at, piece)], out.at[pl.ds(at, piece)], send.at[2, k], recv.at[2, k],
            device_id={"row": row}, device_id_type=MESH_ID)
        copy.start()
        third.append(copy)
    if extra is not None:
        over_col.wait_recv()
        extra_out[...] = pair[...] + got_extra[1]
        over_row.wait_send()
        over_col.wait_send()
    for k in range(PIECES):
        third[k].wait_recv()
        for copy in (first[k], second[k], third[k]):
            copy.wait_send()


def group_sum(part, extra=None):
    rows, width = part.shape
    half = rows // lax.axis_size("row")
    vmem = pl.BlockSpec(memory_space=pltpu.VMEM)
    out_shape = [jax.ShapeDtypeStruct((rows, width), F32)]
    scratch = [pltpu.VMEM((half, width), F32), pltpu.VMEM((half, width), BF),
               pltpu.VMEM((half, width), BF)]
    args = [part]
    if extra is not None:
        args.append(extra)
        out_shape.append(jax.ShapeDtypeStruct(extra.shape, F32))
        scratch += [pltpu.VMEM(extra.shape, F32), pltpu.VMEM((2,) + extra.shape, F32)]
    result = pl.pallas_call(
        reduce_body,
        out_shape=out_shape,
        in_specs=[vmem] * len(args),
        out_specs=[vmem] * len(out_shape),
        scratch_shapes=scratch + [
            pltpu.SemaphoreType.DMA((4, PIECES)), pltpu.SemaphoreType.DMA((4, PIECES))],
        compiler_params=pltpu.CompilerParams(
            collective_id=0 if extra is None else 2, has_side_effects=True),
        name="group_sum",
    )(*args)
    return result[0] if extra is None else result


def gather_body(x, cot, vec, x_out, cot_out, vec_out, send, recv):
    half, width = x.shape
    row, col = greet()
    my_rows = pl.ds(pl.multiple_of((1 - row) * half, half), half)
    my_cols = pl.ds(pl.multiple_of((1 - col) * width, width), width)
    their_cols = pl.ds(pl.multiple_of(col * width, width), width)
    every = pl.ds(0, vec.shape[0])
    jobs = [(x, x_out, my_rows), (vec, vec_out, every), (cot, cot_out, my_rows)]
    copies = []
    first = []
    for k, (own, out, rows) in enumerate(jobs):
        copy = pltpu.make_async_remote_copy(
            own, out.at[rows, my_cols], send.at[0, k], recv.at[0, k],
            device_id={"col": col}, device_id_type=MESH_ID)
        copy.start()
        first.append(copy)
    for k, (own, out, rows) in enumerate(jobs):
        if rows is my_rows:
            copy = pltpu.make_async_remote_copy(
                own, out.at[rows, my_cols], send.at[1, k], recv.at[1, k],
                device_id={"row": row}, device_id_type=MESH_ID)
            copy.start()
            copies.append(copy)
    for own, out, rows in jobs:
        out[rows, my_cols] = own[...]
    for k, (own, out, rows) in enumerate(jobs):
        first[k].wait_recv()
        if rows is my_rows:
            copy = pltpu.make_async_remote_copy(
                out.at[rows, their_cols], out.at[rows, their_cols], send.at[2, k], recv.at[2, k],
                device_id={"row": row}, device_id_type=MESH_ID)
            copy.start()
            copies.append(copy)
    for copy in copies:
        copy.wait_recv()
    for copy in first + copies:
        copy.wait_send()


def group_gather(x, cot, vec):
    half, width = x.shape
    rows, wide = half * lax.axis_size("row"), width * lax.axis_size("col")
    vmem = pl.BlockSpec(memory_space=pltpu.VMEM)
    return pl.pallas_call(
        gather_body,
        out_shape=[
            jax.ShapeDtypeStruct((rows, wide), x.dtype),
            jax.ShapeDtypeStruct((rows, wide), cot.dtype),
            jax.ShapeDtypeStruct((vec.shape[0], wide), vec.dtype),
        ],
        in_specs=[vmem] * 3,
        out_specs=[vmem] * 3,
        scratch_shapes=[pltpu.SemaphoreType.DMA((3, 3)), pltpu.SemaphoreType.DMA((3, 3))],
        compiler_params=pltpu.CompilerParams(collective_id=1, has_side_effects=True),
        name="group_gather",
    )(x, cot, vec)


def ring_body(n, per, q_in, m_in, part, q_out, m_out, y_out, q_got, m_got, q_swap, m_swap, y_row, y_send, y_col, send, recv, swap_send, swap_recv):
    layers = q_in.shape[0]
    cut = m_in.shape[2] // 2
    here = lax.axis_index("dp")
    odd = lax.rem(here, 2)
    pos = here // 2 + odd * (n - 1 - 2 * (here // 2))
    mine = lax.axis_index("col")
    other = 1 - mine

    def device(place):
        late = place // (n // 2)
        return 2 * (place + late * (n - 1 - 2 * place)) + late

    nexts = device(lax.rem(pos + 1, n))
    prevs = device(lax.rem(pos + n - 1, n))
    targets = (nexts, prevs)
    barrier = pltpu.get_barrier_semaphore()
    pl.semaphore_signal(barrier, inc=1, device_id={"dp": nexts}, device_id_type=MESH_ID)
    pl.semaphore_signal(barrier, inc=1, device_id={"dp": prevs}, device_id_type=MESH_ID)
    pl.semaphore_signal(barrier, inc=1, device_id={"col": other}, device_id_type=MESH_ID)
    row = lax.axis_index("row")
    pl.semaphore_signal(barrier, inc=1, device_id={"row": 1 - row}, device_id_type=MESH_ID)
    pl.semaphore_wait(barrier, 4)
    half, wide = y_out.shape
    own_rows = pl.ds(pl.multiple_of(row * half, half), half)
    their_rows = pl.ds(pl.multiple_of((1 - row) * half, half), half)
    own_cols = pl.ds(pl.multiple_of(mine * wide, wide), wide)
    their_cols = pl.ds(pl.multiple_of(other * wide, wide), wide)
    y_over_row = pltpu.make_async_remote_copy(
        part.at[their_rows], y_row, swap_send.at[0, 2], swap_recv.at[0, 2],
        device_id={"row": 1 - row}, device_id_type=MESH_ID)
    y_over_col = pltpu.make_async_remote_copy(
        y_send, y_col, swap_send.at[1, 2], swap_recv.at[1, 2],
        device_id={"col": other}, device_id_type=MESH_ID)

    def chunk(d, back):
        sign = 1 if d % 2 == 0 else -1
        return lax.rem(pos - sign * back + 2 * n, n)

    def view(q, m, p):
        return q if p == 0 else m.at[pl.ds((p - 1) * cut, cut)]

    started = []

    def go(src, dst, d, p, step):
        copy = pltpu.make_async_remote_copy(
            src, dst, send.at[d, p, step], recv.at[d, p, step],
            device_id={"dp": targets[d % 2]}, device_id_type=MESH_ID)
        copy.start()
        started.append(copy)
        return copy

    flight = {}
    for p in range(3):
        for d in range(layers):
            at = chunk(d, 0)
            flight[d, p] = go(
                view(q_in.at[d, :, at], m_in.at[d, at], p),
                view(q_got.at[d, 0], m_got.at[d, 0], p), d, p, 0)
    y_over_row.start()
    for step in range(n - 1):
        if step == 1:
            y_over_row.wait_recv()
            y_send[...] = (part[own_rows, their_cols] + y_row[:, their_cols]).astype(BF)
            y_over_col.start()
        if step == 4:
            y_over_col.wait_recv()
            y_out[...] = part[own_rows, own_cols] + y_row[:, own_cols] + y_col[...].astype(F32)
            y_over_row.wait_send()
            y_over_col.wait_send()
        for p in range(3):
            for d in range(layers):
                flight[d, p].wait_recv()
                own = chunk(d, step + 1)
                if p == 0:
                    q_got[d, step] = (q_got[d, step].astype(F32) + q_in[d, :, own].astype(F32)).astype(BF)
                else:
                    rows = pl.ds((p - 1) * cut, cut)
                    m_got[d, step, rows] = (
                        m_got[d, step, rows].astype(F32) + m_in[d, own, rows].astype(F32)).astype(BF)
                if step < n - 2:
                    flight[d, p] = go(
                        view(q_got.at[d, step], m_got.at[d, step], p),
                        view(q_got.at[d, step + 1], m_got.at[d, step + 1], p), d, p, step + 1)
    last = n - 2
    swaps = []
    for d in range(layers):
        rows = pl.ds(pl.multiple_of(other * per, per), per)
        one = pltpu.make_async_remote_copy(
            q_got.at[d, last, other], q_swap.at[d], swap_send.at[d, 0], swap_recv.at[d, 0],
            device_id={"col": other}, device_id_type=MESH_ID)
        two = pltpu.make_async_remote_copy(
            m_got.at[d, last, rows], m_swap.at[d], swap_send.at[d, 1], swap_recv.at[d, 1],
            device_id={"col": other}, device_id_type=MESH_ID)
        one.start()
        two.start()
        swaps.append((one, two))
    mine_rows = pl.ds(pl.multiple_of(mine * per, per), per)
    other_rows = pl.ds(pl.multiple_of(other * per, per), per)
    rest = pl.ds(2 * per, m_in.shape[2] - 2 * per)
    for d in range(layers):
        at = chunk(d, n - 1)
        q_out[d, at, mine] = q_got[d, last, mine]
        m_out[d, at, mine_rows] = m_got[d, last, mine_rows]
        m_out[d, at, rest] = m_got[d, last, rest]
    for d in range(layers):
        at = chunk(d, n - 1)
        swaps[d][0].wait_recv()
        q_out[d, at, other] = q_swap[d]
        swaps[d][1].wait_recv()
        m_out[d, at, other_rows] = m_swap[d]
    for p in range(3):
        for d in range(layers):
            at = chunk(d, n - 1)
            spot = view(q_out.at[d, at], m_out.at[d, at], p)
            flight[d, p] = go(spot, spot, d, p, n - 1)
    for step in range(n - 1):
        for p in range(3):
            for d in range(layers):
                flight[d, p].wait_recv()
                if step < n - 2:
                    at = chunk(d, step)
                    spot = view(q_out.at[d, at], m_out.at[d, at], p)
                    flight[d, p] = go(spot, spot, d, p, n + step)
    for pair in swaps:
        for copy in pair:
            copy.wait_send()
    for copy in started:
        copy.wait_send()


def ring_sum(q, m, part):
    layers, _, n, per, width = q.shape
    half = part.shape[0] // lax.axis_size("row")
    wide = part.shape[1] // lax.axis_size("col")
    vmem = pl.BlockSpec(memory_space=pltpu.VMEM)
    return pl.pallas_call(
        lambda *refs: ring_body(n, per, *refs),
        out_shape=[
            jax.ShapeDtypeStruct((layers, n, 2, per, width), BF), jax.ShapeDtypeStruct(m.shape, BF),
            jax.ShapeDtypeStruct((half, wide), F32)],
        in_specs=[vmem] * 3,
        out_specs=[vmem] * 3,
        scratch_shapes=[
            pltpu.VMEM((layers, n - 1, 2, per, width), BF),
            pltpu.VMEM((layers, n - 1) + m.shape[2:], BF),
            pltpu.VMEM((layers, per, width), BF),
            pltpu.VMEM((layers, per, m.shape[3]), BF),
            pltpu.VMEM((half, part.shape[1]), F32),
            pltpu.VMEM((half, wide), BF),
            pltpu.VMEM((half, wide), BF),
            pltpu.SemaphoreType.DMA((layers, 3, 2 * n)),
            pltpu.SemaphoreType.DMA((layers, 3, 2 * n)),
            pltpu.SemaphoreType.DMA((layers, 3)),
            pltpu.SemaphoreType.DMA((layers, 3)),
        ],
        compiler_params=pltpu.CompilerParams(
            collective_id=3, has_side_effects=True, vmem_limit_bytes=60 * 1024 * 1024),
        name="ring_sum",
    )(q, m, part)


def make_scores(query, key, allowed):
    scores = jnp.einsum("hqd,hkd->hqk", query, key, preferred_element_type=F32) * SCALE
    return jnp.where(allowed[None], scores, NEG)


def swap_col(value):
    return lax.ppermute(value, "col", [(0, 1), (1, 0)])


def columns_whole(own, gate):
    col = lax.axis_index("col")
    depth, width = own.shape[1], own.shape[2] // 2
    later = (gate.reshape(-1)[0].astype(F32) * 0.0).astype(jnp.int32)
    got = swap_col(lax.dynamic_slice_in_dim(own, (1 - col) * width + later, width, 2))
    kept = lax.dynamic_slice_in_dim(own, col * width, width, 2)
    low = jnp.where(col == 0, kept, got)
    high = jnp.where(col == 0, got, kept)
    return jnp.concatenate([low, high], axis=1)


def rows_whole(grad):
    col = lax.axis_index("col")
    depth = grad.shape[0] // 2
    got = swap_col(lax.dynamic_slice_in_dim(grad, (1 - col) * depth, depth, 0))
    kept = lax.dynamic_slice_in_dim(grad, col * depth, depth, 0)
    low = jnp.where(col == 0, kept, got)
    high = jnp.where(col == 0, got, kept)
    return jnp.concatenate([low, high], axis=1)


def forward_layer(state, allowed, cosine, sine, params):
    gain1, bias1, gain2, bias2, w_qkv, b_qkv, w_up, b_up, w_out, w_down, b_both = params
    width = state.shape[1]
    mean = jnp.sum(state, axis=1, keepdims=True) / width
    squares = jnp.sum(state * state, axis=1, keepdims=True) / width
    inverse = lax.rsqrt(squares - mean * mean + EPS)
    normed = (state - mean) * inverse
    first = (normed * gain1 + bias1).astype(BF)
    second = (normed * gain2 + bias2).astype(BF)
    rows = state.shape[0]
    qkv = (jnp.dot(first, w_qkv, preferred_element_type=F32) + b_qkv).reshape(rows, -1, 3, HD)
    query = rotate(qkv[:, :, 0], cosine, sine).astype(BF).transpose(1, 0, 2)
    key = rotate(qkv[:, :, 1], cosine, sine).astype(BF).transpose(1, 0, 2)
    value = qkv[:, :, 2].astype(BF).transpose(1, 0, 2)
    scores = make_scores(query, key, allowed)
    top = jnp.max(scores, axis=-1, keepdims=True)
    lse = top + jnp.log(jnp.sum(jnp.exp(scores - top), axis=-1, keepdims=True))
    probs = jnp.exp(scores - lse).astype(BF)
    mixed = jnp.einsum("hqk,hkd->qhd", probs, value, preferred_element_type=F32)
    mixed = mixed.astype(BF).reshape(rows, -1)
    up = jnp.dot(second, w_up, preferred_element_type=F32) + b_up
    act = gelu_exact(up).astype(BF)
    part = jnp.dot(mixed, w_out, preferred_element_type=F32) + jnp.dot(
        act, w_down, preferred_element_type=F32)
    return part, (normed, inverse, first, second, query, key, value, mixed, lse, up, act)


def backward_layer(grad, allowed, cosine, sine, params, cache):
    gain1, bias1, gain2, bias2, w_qkv, b_qkv, w_up, b_up, w_out, w_down, b_both = params
    normed, inverse, first, second, query, key, value, mixed, lse, up, act = cache
    rows, width = grad.shape
    grad_b = grad.astype(BF)
    g_bout = jnp.sum(grad, axis=0)
    grad_mixed = jnp.einsum("td,kd->tk", grad_b, w_out, preferred_element_type=F32).astype(BF)
    grad_act = jnp.einsum("td,kd->tk", grad_b, w_down, preferred_element_type=F32)
    grad_up = grad_act * gelu_slope(up)
    g_bup = jnp.sum(grad_up, axis=0)
    grad_up_b = grad_up.astype(BF)
    scores = make_scores(query, key, allowed)
    probs = jnp.exp(scores - lse)
    grad_heads = grad_mixed.reshape(rows, -1, HD).transpose(1, 0, 2)
    mixed_heads = mixed.reshape(rows, -1, HD).transpose(1, 0, 2)
    delta = jnp.sum(grad_heads.astype(F32) * mixed_heads.astype(F32), axis=-1, keepdims=True)
    grad_value = jnp.einsum("hqk,hqd->khd", probs.astype(BF), grad_heads, preferred_element_type=F32)
    grad_probs = jnp.einsum("hqd,hkd->hqk", grad_heads, value, preferred_element_type=F32)
    grad_scores = (probs * (grad_probs - delta) * SCALE).astype(BF)
    grad_query = jnp.einsum("hqk,hkd->qhd", grad_scores, key, preferred_element_type=F32)
    grad_key = jnp.einsum("hqk,hqd->khd", grad_scores, query, preferred_element_type=F32)
    grad_query = unrotate(grad_query, cosine, sine)
    grad_key = unrotate(grad_key, cosine, sine)
    grad_qkv = jnp.stack([grad_query, grad_key, grad_value], axis=2).reshape(rows, -1)
    g_bqkv = jnp.sum(grad_qkv, axis=0)
    grad_qkv_b = grad_qkv.astype(BF)
    part_first = jnp.einsum("tn,dn->td", grad_qkv_b, w_qkv, preferred_element_type=F32)
    part_second = jnp.einsum("tn,dn->td", grad_up_b, w_up, preferred_element_type=F32)
    part = part_first * gain1 + part_second * gain2
    g_wout = jnp.einsum("tk,td->kd", mixed, grad_b, preferred_element_type=F32)
    g_wdown = jnp.einsum("tk,td->kd", act, grad_b, preferred_element_type=F32)
    g_wqkv = jnp.einsum("td,tn->dn", first, grad_qkv_b, preferred_element_type=F32)
    g_wup = jnp.einsum("td,tn->dn", second, grad_up_b, preferred_element_type=F32)
    shares = lax.axis_size("row") * lax.axis_size("col")
    narrow = jnp.concatenate([
        jnp.stack([
            jnp.sum(part_first * normed, axis=0), jnp.sum(part_first, axis=0),
            jnp.sum(part_second * normed, axis=0), jnp.sum(part_second, axis=0),
            g_bout / shares,
        ]),
        jnp.zeros((3, width), F32),
    ])
    grad_norm, narrow = group_sum(part, narrow)
    centred = (
        grad_norm
        - jnp.sum(grad_norm, axis=1, keepdims=True) / width
        - normed * (jnp.sum(grad_norm * normed, axis=1, keepdims=True) / width)
    )
    grad_x = grad + inverse * centred
    heavy = (g_wqkv.astype(BF), g_wup.astype(BF), g_wout.astype(BF), g_wdown.astype(BF))
    return grad_x, heavy, (g_bqkv, g_bup), narrow


def per_device(
    x_in, cotangent, segment_ids, norm1_gain, norm1_bias, norm2_gain, norm2_bias,
    w_qkv, b_qkv, w_up, b_up, w_out, b_out, w_down, b_down,
):
    half, part_width = x_in.shape
    row = lax.axis_index("row")
    col = lax.axis_index("col")
    length = segment_ids.shape[1]
    layers = w_qkv.shape[0]
    cosine, sine = rope_tables(length)
    places = jnp.arange(length, dtype=jnp.int32)
    labels = segment_ids[0]
    allowed = (places[:, None] >= places[None, :]) & (labels[:, None] == labels[None, :])
    vec = jnp.stack([norm1_gain, norm1_bias, norm2_gain, norm2_bias, b_out + b_down])
    vec = vec.reshape(-1, part_width)
    pad = -vec.shape[0] % 8
    state_in, cot, vec = group_gather(x_in, cotangent.astype(BF), jnp.pad(vec, ((0, pad), (0, 0))))
    grad_in = cot.astype(F32)
    vectors = vec[: vec.shape[0] - pad].reshape(5, layers, -1)
    wide_qkv, wide_up, gate = [], [], vec
    for l in range(layers):
        wide_qkv.append(columns_whole(w_qkv[l : l + 1], gate)[0])
        wide_up.append(columns_whole(w_up[l : l + 1], gate)[0])
        gate = wide_qkv[-1]

    def own(whole):
        return lax.dynamic_slice(whole, (row * half, col * part_width), (half, part_width))

    params = [
        (vectors[0, l], vectors[1, l], vectors[2, l], vectors[3, l], wide_qkv[l], b_qkv[l],
         wide_up[l], b_up[l], w_out[l], w_down[l], vectors[4, l])
        for l in range(layers)
    ]
    state = state_in
    caches = []
    for layer in range(layers):
        part, cache = forward_layer(state, allowed, cosine, sine, params[layer])
        caches.append(cache)
        if layer < layers - 1:
            state = state + group_sum(part) + params[layer][-1]
    y_base = x_in + own(state - state_in + params[-1][-1])
    grad = grad_in
    heavy = [None] * layers
    thin = [None] * layers
    narrow = [None] * layers
    for layer in reversed(range(layers)):
        grad, heavy[layer], thin[layer], narrow[layer] = backward_layer(
            grad, allowed, cosine, sine, params[layer], caches[layer])
    x_grad = cotangent + own(grad - grad_in)
    n = lax.axis_size("dp")
    width = state.shape[1]
    per = width // 2 // n
    if per % 16 == 0 and (w_out.shape[1] // n) % 8 == 0 and layers == 2:
        q = jnp.stack([h[0].reshape(2, n, per, -1) for h in heavy])
        blocks = []
        for layer in range(layers):
            g_bqkv, g_bup = thin[layer]
            g_bqkv = jnp.pad(g_bqkv, (0, width - g_bqkv.shape[0]))
            small = jnp.concatenate([narrow[layer][:5], g_bqkv[None], g_bup.reshape(-1, width)])
            small = jnp.pad(small, ((0, 8 - small.shape[0]), (0, 0))).astype(BF)
            small = jnp.pad(small[None], ((0, n - 1), (0, 0), (0, 0)))
            _, b, c, d = heavy[layer]
            blocks.append(jnp.concatenate([
                b[: width // 2].reshape(n, per, -1), b[width // 2 :].reshape(n, per, -1),
                d.reshape(n, -1, width), c.reshape(n, -1, width), small], axis=1))
        q, m, y_sum = ring_sum(q, jnp.stack(blocks), part)
        y_out = y_base + y_sum
        deep = w_down.shape[1] // n
        flat = w_out.shape[1] // n
        g_wqkv = jnp.concatenate(
            [q[:, :, k].reshape(layers, width // 2, -1).astype(F32) for k in range(2)], axis=2)
        g_wup = jnp.concatenate(
            [m[:, :, k * per : (k + 1) * per].reshape(layers, width // 2, -1).astype(F32)
             for k in range(2)], axis=2)
        g_wdown = m[:, :, 2 * per : 2 * per + deep].reshape(w_down.shape).astype(F32)
        g_wout = m[:, :, 2 * per + deep : 2 * per + deep + flat].reshape(w_out.shape).astype(F32)
        small = m[:, 0, 2 * per + deep + flat :].astype(F32)
        narrow = small[:, :5]
        g_bqkv = small[:, 5, : b_qkv.shape[1]]
        g_bup = small[:, 6].reshape(b_up.shape)
    else:
        y_out = y_base + own(group_sum(part))
        summed = []
        for layer in range(layers):
            a, b, c, d = heavy[layer]
            summed.append(lax.psum((rows_whole(a), rows_whole(b), c, d), "dp"))
        g_bqkv, g_bup, narrow = lax.psum((
            jnp.stack([t[0] for t in thin]), jnp.stack([t[1] for t in thin]),
            jnp.stack([t[:5] for t in narrow])), "dp")
        g_wqkv, g_wup, g_wout, g_wdown = (
            jnp.stack([h[k] for h in summed]).astype(F32) for k in range(4))
    narrow = lax.dynamic_slice_in_dim(narrow, col * part_width, part_width, 2)
    g_bout = narrow[:, 4]
    return (
        y_out, x_grad, narrow[:, 0], narrow[:, 1], narrow[:, 2], narrow[:, 3],
        g_wqkv, g_bqkv, g_wup, g_bup, g_wout, g_bout, g_wdown, g_bout,
    )


def solution(mesh):
    in_specs = (
        P(("dp", "row"), "col"),
        P(("dp", "row"), "col"),
        P("dp", None),
        P(None, "col"),
        P(None, "col"),
        P(None, "col"),
        P(None, "col"),
        P(None, "col", "row"),
        P(None, ("row", "col")),
        P(None, "col", "row"),
        P(None, ("row", "col")),
        P(None, ("row", "col"), None),
        P(None, "col"),
        P(None, ("row", "col"), None),
        P(None, "col"),
    )
    out_specs = (
        P(("dp", "row"), "col"),
        P(("dp", "row"), "col"),
        P(None, "col"),
        P(None, "col"),
        P(None, "col"),
        P(None, "col"),
        P(None, "col", "row"),
        P(None, ("row", "col")),
        P(None, "col", "row"),
        P(None, ("row", "col")),
        P(None, ("row", "col"), None),
        P(None, "col"),
        P(None, ("row", "col"), None),
        P(None, "col"),
    )
    return jax.shard_map(
        per_device, mesh=mesh, in_specs=in_specs, out_specs=out_specs, check_vma=False
    )
```
